32 devices in a mesh: parts: 2 (over y), tensor: 4 (over z), dp: 4 (over x, core).
Axes of the slice: x: 2, y: 2, z: 4, core: 2. Of those that a mesh axis runs over, the one named last changes fastest.
Arguments:
- inputs: bfloat16 [4096, 8192], P(('parts', 'dp'), 'tensor'), parts along dimension 0, may hold values from -6 to 6
- cotangent: bfloat16 [4096, 8192], P(('parts', 'dp'), 'tensor'), parts along dimension 0, may hold values from -6 to 6
- weight: bfloat16 [8192, 8192], P(None, 'tensor'), may hold values from -0.0625 to 0.0625
- down_weight_maps: bfloat16 [8192, 2048], P('tensor', 'parts'), parts along dimension 1, may hold values from -0.0625 to 0.0625
- up_weight_maps: bfloat16 [2048, 8192], P('parts', 'tensor'), parts along dimension 0, may hold values from -0.75 to 0.75
- counts: int32 [8, 16], P('parts'), parts along dimension 0, may hold values from 0 to 256, as said below
- ranks: int32 [32], P('parts'), parts along dimension 0, may hold values from 8 to 64, as said below
- owners: int32 [32], P('parts'), parts along dimension 0, may hold values from 0 to 3
Outputs:
- projected: bfloat16 [4096, 8192], P(('parts', 'dp'), 'tensor'), parts along dimension 0
- input_grad: bfloat16 [4096, 8192], P(('parts', 'dp'), 'tensor'), parts along dimension 0
- grad_a: float32 [8, 8192, 1024], P(('parts', 'dp'), 'tensor'), parts along dimension 0
- grad_b: float32 [8, 1024, 8192], P(('parts', 'dp'), None, 'tensor'), parts along dimension 0
The draws below stay inside these ranges and needn't reach their ends.
There are 2 independent parts, one for each index of `parts`. The reference program is written for one: setup_inputs(seed, part) draws one part's arguments, and reference() takes and returns one part's arrays. A program takes and returns all parts, laid end to end along the dimension named above; an argument that names none is the same for every part. Nothing has to cross between parts.
Inputs may be any that keep to these rules, and one draw needn't show every extreme that they name: `counts`: each row sums to at most 512, one row to exactly 512, and all rows together to exactly 1024; some entry is exactly 256. `ranks`: each rank is 64 divided by 1, 2, 4 or 8; some trial has 64 and some 64 // 8.
All inputs are finite; a program needn't handle non-finite values.
Results may differ from the reference program's by a relative error of at most 0.0034.
Values may be sent and summed in bfloat16 or wider, within the bound.
A program may use at most 256 MiB of HBM per device.

```python
import jax
import jax.numpy as jnp

MODEL_WIDTH = 8192
LARGEST_RANK = 64
TRIALS = 16
R_DEV = 512
DP_GROUPS = 4
ROWS = 2048
TOTAL_RANK_COLS = 1024


def split_half(key, halves, pieces):
    raw = jax.random.randint(key, (DP_GROUPS, pieces - 1), 0, 1 << 20)
    inner = jnp.sort(raw % (halves[:, None] + 1), axis=1).astype(jnp.int32)
    bounds = jnp.concatenate([jnp.zeros((DP_GROUPS, 1), jnp.int32), inner, halves[:, None]], axis=1)
    return (bounds[:, 1:] - bounds[:, :-1]).astype(jnp.int32)


def draw_counts(key, part):
    key_full, key_cuts, key_first, key_second, key_pick = jax.random.split(jax.random.fold_in(key, 11), 5)
    full_group = jax.random.randint(key_full, (), 0, DP_GROUPS)
    remain = DP_GROUPS * R_DEV // 2 - R_DEV
    cut_points = jnp.sort(jax.random.randint(key_cuts, (DP_GROUPS - 2,), 0, remain + 1))
    edges = jnp.concatenate([jnp.zeros((1,), jnp.int32), cut_points.astype(jnp.int32), jnp.full((1,), remain, jnp.int32)])
    others = edges[1:] - edges[:-1]
    group_ids = jnp.arange(DP_GROUPS, dtype=jnp.int32)
    other_index = jnp.clip(group_ids - (group_ids > full_group).astype(jnp.int32), 0, DP_GROUPS - 2)
    totals = jnp.where(group_ids == full_group, R_DEV, jnp.take(others, other_index)).astype(jnp.int32)
    half_count = TRIALS // 2
    first_half = (totals // 2).astype(jnp.int32)
    second_half = (totals - first_half).astype(jnp.int32)
    part_one = split_half(key_first, first_half, half_count)
    part_two = split_half(key_second, second_half, TRIALS - half_count)
    pick = jax.random.randint(key_pick, (), 0, half_count)
    single = jnp.where(jnp.arange(half_count, dtype=jnp.int32) == pick, R_DEV // 2, 0).astype(jnp.int32)
    part_one = jnp.where((group_ids == full_group)[:, None], single[None, :], part_one)
    return jnp.concatenate([part_one, part_two], axis=1).astype(jnp.int32)


def draw_ranks(key, part):
    key_level, key_order = jax.random.split(jax.random.fold_in(key, 23))
    levels = jax.random.randint(key_level, (TRIALS,), 0, 4).astype(jnp.int32)
    values = jnp.right_shift(jnp.full((TRIALS,), LARGEST_RANK, jnp.int32), levels)
    order = jax.random.permutation(key_order, TRIALS)
    values = values.at[order[0]].set(LARGEST_RANK).at[order[1]].set(LARGEST_RANK // 8)
    return values.astype(jnp.int32)


def touch_ends(entries, key, low, high):
    index_at = [jax.random.randint(jax.random.fold_in(key, axis), (), 0, length) for axis, length in enumerate(entries.shape)]
    longest = entries.shape.index(max(entries.shape))
    beside = index_at[:longest] + [(index_at[longest] + 1) % entries.shape[longest]] + index_at[longest + 1:]
    return entries.at[tuple(index_at)].set(low).at[tuple(beside)].set(high)


def shard_levels(key, extent, shards, low, top_value):
    factor_of, own = 1.0, jax.random.fold_in(key, 6)
    for dim, shards_of in shards:
        heights = jnp.exp(jax.random.uniform(jax.random.fold_in(own, dim), (shards_of,), jnp.float32, low / len(shards), top_value / len(shards)))
        factor_of = factor_of * jnp.repeat(heights, extent[dim] // shards_of).reshape([-1 if axis == dim else 1 for axis in range(len(extent))])
    return factor_of


def normal_values(stream_key, dims, deviation, bound, shards=(), kind=jnp.bfloat16):
    values = jax.random.normal(stream_key, dims, jnp.float32) * deviation
    if len(shards) > 0:
        values = shard_levels(stream_key, dims, shards, -0.22, 0.18) * values
    return jnp.clip(values, min=-bound, max=bound).astype(kind)


def setup_inputs(seed: int = 0, part: int = 0) -> dict:
    arg_keys = jax.random.split(jax.random.key(seed), 9)
    own_keys = jax.random.split(jax.random.fold_in(arg_keys[8], part), 9)
    return {
        "inputs": normal_values(own_keys[0], (ROWS, MODEL_WIDTH), 1.0, 6.0, ((0, 4), (1, 4))),
        "cotangent": normal_values(own_keys[1], (ROWS, MODEL_WIDTH), 1.0, 6.0, ((0, 4), (1, 4))),
        "weight": normal_values(arg_keys[2], (MODEL_WIDTH, MODEL_WIDTH), MODEL_WIDTH ** -0.5, 0.0625, ((1, 4),)),
        "down_weight_maps": normal_values(own_keys[3], (MODEL_WIDTH, TOTAL_RANK_COLS), MODEL_WIDTH ** -0.5, 0.0625, ((0, 4),)),
        "up_weight_maps": normal_values(own_keys[4], (TOTAL_RANK_COLS, MODEL_WIDTH), LARGEST_RANK ** -0.5, 0.75, ((1, 4),)),
        "counts": draw_counts(jax.random.fold_in(jax.random.fold_in(arg_keys[8], part), 71), part),
        "ranks": draw_ranks(jax.random.fold_in(jax.random.fold_in(arg_keys[8], part), 71), part),
        "owners": touch_ends(jax.random.randint(own_keys[7], (TRIALS,), 0, DP_GROUPS), jax.random.fold_in(own_keys[7], 1), 0, DP_GROUPS - 1).astype(jnp.int32),
    }


adapter_alpha = 16.0


def reference(inputs, cotangent, weight, down_weight_maps, up_weight_maps, counts, ranks, owners):
    slot_ids = jnp.arange(ROWS, dtype=jnp.int32)
    group_of = slot_ids // R_DEV
    within = slot_ids % R_DEV
    cumulative = jnp.cumsum(counts, axis=1).astype(jnp.int32)
    bounds = jnp.take(cumulative, group_of, axis=0)
    trial_of = jnp.sum((within[:, None] >= bounds).astype(jnp.int32), axis=1)
    is_live = trial_of < TRIALS
    column = jnp.arange(TOTAL_RANK_COLS, dtype=jnp.int32)
    col_trial = column // LARGEST_RANK
    column_slot = column % LARGEST_RANK
    rank_per_column = jnp.take(ranks, col_trial)
    scale_per_column = jnp.where(column_slot < rank_per_column, adapter_alpha / rank_per_column.astype(jnp.float32), jnp.float32(0.0))
    coef = jnp.where(trial_of[:, None] == col_trial[None, :], scale_per_column[None, :], jnp.float32(0.0))
    down_projected = jnp.dot(inputs, down_weight_maps, preferred_element_type=jnp.float32)
    scaled_down_projected = (coef * down_projected).astype(jnp.bfloat16)
    projected = jnp.dot(inputs, weight, preferred_element_type=jnp.float32) + jnp.dot(scaled_down_projected, up_weight_maps, preferred_element_type=jnp.float32)
    projected = jnp.where(is_live[:, None], projected, jnp.float32(0.0)).astype(jnp.bfloat16)
    up_projected = jnp.dot(cotangent, up_weight_maps.T, preferred_element_type=jnp.float32)
    scaled_up_projected = (coef * up_projected).astype(jnp.bfloat16)
    input_gradient = jnp.dot(cotangent, weight.T, preferred_element_type=jnp.float32) + jnp.dot(scaled_up_projected, down_weight_maps.T, preferred_element_type=jnp.float32)
    input_grad = jnp.where(is_live[:, None], input_gradient, jnp.float32(0.0)).astype(jnp.bfloat16)
    trial_rows = jnp.sum(counts, axis=0)
    inverse = jnp.float32(1.0) / jnp.maximum(trial_rows, 1).astype(jnp.float32)
    inverse_col = jnp.take(inverse, col_trial)
    full_a = jnp.dot(inputs.T, scaled_up_projected, preferred_element_type=jnp.float32) * inverse_col[None, :]
    full_b = jnp.dot(scaled_down_projected.T, cotangent, preferred_element_type=jnp.float32) * inverse_col[:, None]
    owner_col = jnp.take(owners, col_trial)
    owned = (owner_col[None, :] == jnp.arange(DP_GROUPS, dtype=jnp.int32)[:, None]).astype(jnp.float32)
    grad_a = owned[:, None, :] * full_a[None, :, :]
    grad_b = owned[:, :, None] * full_b[None, :, :]
    return (projected, input_grad, grad_a, grad_b)
```

```python
import jax
import jax.numpy as jnp
from jax import lax
from jax.sharding import PartitionSpec as P

LARGEST_RANK = 64
TRIALS = 16
LANES = 128

adapter_alpha = 16.0

TRAILING = (((1,), (1,)), ((), ()))
FIRST = (((0,), (0,)), ((), ()))


def fold_columns(values, match):
    width = values.shape[1]
    kept = jnp.where(match, values, 0.0)
    return sum(kept[:, i : i + LANES] for i in range(0, width, LANES))


def spread_columns(folded, match):
    repeats = match.shape[1] // LANES
    return jnp.where(match, jnp.concatenate([folded] * repeats, axis=1), jnp.zeros((), folded.dtype))


def local(inputs, cotangent, weight, down_weight_maps, up_weight_maps, counts, ranks, owners):
    slot_count, feature_local = inputs.shape
    group_count = counts.shape[0]
    width = down_weight_maps.shape[1]
    column = jnp.arange(width, dtype=jnp.int32)
    col_trial = column // LARGEST_RANK
    column_slot = column % LARGEST_RANK
    trial_ids = jnp.arange(TRIALS, dtype=jnp.int32)
    matches = col_trial[:, None] == trial_ids[None, :]
    rank_per_column = jnp.sum(jnp.where(matches, ranks[None, :], 0), axis=1)
    owner_col = jnp.sum(jnp.where(matches, owners[None, :], 0), axis=1)
    scale_per_column = jnp.where(
        column_slot < rank_per_column, adapter_alpha / rank_per_column.astype(jnp.float32), 0.0
    )
    trial_rows = jnp.sum(counts, axis=0)
    per_trial = 1.0 / jnp.maximum(trial_rows, 1).astype(jnp.float32)
    inverse_col = jnp.sum(jnp.where(matches, per_trial[None, :], 0.0), axis=1)
    cumulative = jnp.cumsum(counts, axis=1)
    group_ids = jnp.arange(group_count, dtype=jnp.int32)
    my_group = lax.axis_index("dp")
    positions = jnp.arange(slot_count, dtype=jnp.int32)
    trial_all = jnp.sum(
        (positions[None, :, None] >= cumulative[:, None, :]).astype(jnp.int32), axis=2
    )
    row_trial = jnp.sum(jnp.where((group_ids == my_group)[:, None], trial_all, 0), axis=0)
    is_live = row_trial < TRIALS
    match = row_trial[:, None] == col_trial[None, :]
    match_all = trial_all.reshape(-1)[:, None] == col_trial[None, :]
    coef = jnp.where(match, scale_per_column[None, :], 0.0)
    coef_folded = fold_columns(coef, match)

    down_part = jnp.dot(inputs, down_weight_maps, preferred_element_type=jnp.float32)
    back_part = lax.dot_general(
        cotangent, up_weight_maps, TRAILING, preferred_element_type=jnp.float32
    )
    folded = jnp.concatenate([fold_columns(down_part, match), fold_columns(back_part, match)], axis=1)
    folded = lax.psum(folded, "tensor")
    scaled_down_f = (coef_folded * folded[:, :LANES]).astype(jnp.bfloat16)
    scaled_back_f = (coef_folded * folded[:, LANES:]).astype(jnp.bfloat16)

    all_inputs = lax.all_gather(inputs, "tensor", axis=1, tiled=True)
    mine = lax.axis_index("tensor")
    block = jnp.arange(weight.shape[0], dtype=jnp.int32) // feature_local
    frozen_back = lax.dot_general(cotangent, weight, TRAILING, preferred_element_type=jnp.float32)
    others = jnp.where((block == mine)[None, :], 0.0, frozen_back).astype(jnp.bfloat16)
    others_share = lax.psum_scatter(others, "tensor", scatter_dimension=1, tiled=True)
    own_weight = lax.dynamic_slice_in_dim(weight, mine * feature_local, feature_local, 0)
    own_share = lax.dot_general(cotangent, own_weight, TRAILING, preferred_element_type=jnp.float32)
    frozen_share = own_share + others_share.astype(jnp.float32)

    group_inputs = lax.all_gather(inputs, "dp", axis=0, tiled=True)
    group_cotangent = lax.all_gather(cotangent, "dp", axis=0, tiled=True)
    both = lax.all_gather(
        jnp.concatenate([scaled_down_f, scaled_back_f], axis=1), "dp", axis=0, tiled=True
    )

    frozen_output = jnp.dot(all_inputs, weight, preferred_element_type=jnp.float32)
    scaled_down = spread_columns(scaled_down_f, match)
    scaled_back = spread_columns(scaled_back_f, match)
    merged = frozen_output + jnp.dot(scaled_down, up_weight_maps, preferred_element_type=jnp.float32)
    projected = jnp.where(is_live[:, None], merged, 0.0).astype(jnp.bfloat16)
    adapter_in = lax.dot_general(
        scaled_back, down_weight_maps, TRAILING, preferred_element_type=jnp.float32
    )
    input_grad = jnp.where(
        is_live[:, None], frozen_share + adapter_in, 0.0
    ).astype(jnp.bfloat16)

    owned = jnp.where(owner_col == my_group, inverse_col, 0.0)
    down_all = spread_columns(both[:, :LANES], match_all)
    back_all = spread_columns(both[:, LANES:], match_all)
    grad_a = lax.dot_general(group_inputs, back_all, FIRST, preferred_element_type=jnp.float32)
    grad_b = lax.dot_general(down_all, group_cotangent, FIRST, preferred_element_type=jnp.float32)
    grad_a = (grad_a * owned[None, :])[None]
    grad_b = (grad_b * owned[:, None])[None]
    return (projected, input_grad, grad_a, grad_b)


def solution(mesh):
    return jax.shard_map(
        local,
        mesh=mesh,
        in_specs=(
            P(("parts", "dp"), "tensor"),
            P(("parts", "dp"), "tensor"),
            P(None, "tensor"),
            P("tensor", "parts"),
            P("parts", "tensor"),
            P("parts", None),
            P("parts"),
            P("parts"),
        ),
        out_specs=(
            P(("parts", "dp"), "tensor"),
            P(("parts", "dp"), "tensor"),
            P(("parts", "dp"), "tensor", None),
            P(("parts", "dp"), None, "tensor"),
        ),
        check_vma=False,
    )
```

```python
import functools

import jax
import jax.numpy as jnp
from jax import lax
from jax.experimental import pallas as pl
from jax.experimental.pallas import tpu as pltpu
from jax.sharding import PartitionSpec as P

LARGEST_RANK = 64
TRIALS = 16
LANES = 128

adapter_alpha = 16.0

TRAILING = (((1,), (1,)), ((), ()))
FIRST = (((0,), (0,)), ((), ()))


MESH = pl.DeviceIdType.MESH


def exchange_kernel(
    n, chunks, cot_ref, inp_ref, w_ref, share_ref, ginp_ref, gcot_ref,
    cot_v, wbuf, part, to_right, to_left, out_v,
    w_sem, cot_sem, out_sem, own_sem, rs_send, rs_recv, ls_send, ls_recv, dp_send, dp_recv,
):
    me = lax.axis_index("tensor")
    group = lax.axis_index("dp")
    sibling = group + 1 - 2 * lax.rem(group, 2)
    cross = lax.rem(group + 2, 4)
    far = lax.rem(sibling + 2, 4)
    right, left = jnp.minimum(me + 1, n - 1), jnp.maximum(me - 1, 0)
    n_right, n_left = n - 1 - me, me
    width = wbuf.shape[1]
    rows = cot_v.shape[0]
    feat = width * chunks

    def weight_copy(i):
        dest, _, c, _ = item(i)
        start = pl.multiple_of(dest * feat + c * width, width)
        return pltpu.make_async_copy(
            w_ref.at[pl.ds(start, width), :], wbuf.at[lax.rem(i, 2)], w_sem.at[lax.rem(i, 2)]
        )

    def item(i):
        both = jnp.minimum(n_right, n_left)
        paired = 2 * both * chunks
        in_pair = i < paired
        rest = jnp.maximum(i - paired, 0)
        p = jnp.where(in_pair, i // (2 * chunks), both + rest // chunks)
        c = jnp.where(in_pair, lax.rem(i, 2 * chunks) // 2, lax.rem(rest, chunks))
        is_right = jnp.where(in_pair, lax.rem(i, 2), jnp.where(n_right > n_left, 0, 1))
        own = i >= (n - 1) * chunks
        kind = jnp.where(own, 2, is_right)
        dest = jnp.where(own, me, jnp.where(is_right == 0, n - 1 - p, p))
        return dest, p, c, kind

    pltpu.make_async_copy(cot_ref, cot_v, cot_sem).start()
    weight_copy(0).start()

    barrier = pltpu.get_barrier_semaphore()
    for peer in (sibling, cross):
        pl.semaphore_signal(barrier, inc=1, device_id={"dp": peer}, device_id_type=MESH)

    @pl.when(me > 0)
    def _():
        pl.semaphore_signal(barrier, inc=1, device_id={"tensor": left}, device_id_type=MESH)

    @pl.when(me < n - 1)
    def _():
        pl.semaphore_signal(barrier, inc=1, device_id={"tensor": right}, device_id_type=MESH)

    edges = jnp.where(me > 0, 1, 0) + jnp.where(me < n - 1, 1, 0)
    pl.semaphore_wait(barrier, 2 + edges)

    def dp_copy(k, src, dst, slot, peer):
        return pltpu.make_async_remote_copy(
            src_ref=src, dst_ref=dst.at[slot], send_sem=dp_send.at[k], recv_sem=dp_recv.at[k],
            device_id={"dp": peer}, device_id_type=MESH,
        )

    def right_copy(p, c):
        return pltpu.make_async_remote_copy(
            src_ref=to_right.at[p, c], dst_ref=to_right.at[p, c],
            send_sem=rs_send.at[p, c], recv_sem=rs_recv.at[p, c],
            device_id={"tensor": right}, device_id_type=MESH,
        )

    def left_copy(p, c):
        return pltpu.make_async_remote_copy(
            src_ref=to_left.at[p, c], dst_ref=to_left.at[p, c],
            send_sem=ls_send.at[p, c], recv_sem=ls_recv.at[p, c],
            device_id={"tensor": left}, device_id_type=MESH,
        )

    for k, (src, dst) in enumerate(((inp_ref, ginp_ref), (cot_ref, gcot_ref))):
        pltpu.make_async_copy(src, dst.at[group], own_sem.at[k]).start()
        dp_copy(3 * k, src, dst, group, cross).start()
        dp_copy(3 * k + 1, src, dst, group, sibling).start()

    pltpu.make_async_copy(cot_ref, cot_v, cot_sem).wait()

    def step(i, carry):
        dest, p, c, kind = item(i)
        weight_copy(i).wait()

        @pl.when(i + 1 < n * chunks)
        def _():
            weight_copy(i + 1).start()

        part[...] = lax.dot_general(
            cot_v[...], wbuf[lax.rem(i, 2)], TRAILING, preferred_element_type=jnp.float32
        )

        @pl.when(kind == 0)
        def _():
            @pl.when(me > 0)
            def _():
                right_copy(p, c).wait_recv()
                part[...] += to_right[p, c].astype(jnp.float32)

            to_right[p, c] = part[...].astype(jnp.bfloat16)
            right_copy(p, c).start()

        @pl.when(kind == 1)
        def _():
            @pl.when(me < n - 1)
            def _():
                left_copy(p, c).wait_recv()
                part[...] += to_left[p, c].astype(jnp.float32)

            to_left[p, c] = part[...].astype(jnp.bfloat16)
            left_copy(p, c).start()

        @pl.when(kind == 2)
        def _():
            @pl.when(me > 0)
            def _():
                right_copy(n_right, c).wait_recv()
                part[...] += to_right[n_right, c].astype(jnp.float32)

            @pl.when(me < n - 1)
            def _():
                left_copy(n_left, c).wait_recv()
                part[...] += to_left[n_left, c].astype(jnp.float32)

            out_v[c] = part[...]
            start = pl.multiple_of(c * width, width)
            pltpu.make_async_copy(
                out_v.at[c], share_ref.at[:, pl.ds(start, width)], out_sem.at[c]
            ).start()

        return carry

    lax.fori_loop(0, (n - 1) * chunks, step, 0)

    for k, (src, dst) in enumerate(((inp_ref, ginp_ref), (cot_ref, gcot_ref))):
        dp_copy(3 * k, src, dst, cross, cross).wait_recv()
        dp_copy(3 * k + 2, dst.at[cross], dst, cross, sibling).start()

    lax.fori_loop((n - 1) * chunks, n * chunks, step, 0)

    def drain_right(j, carry):
        right_copy(j // chunks, lax.rem(j, chunks)).wait_send()
        return carry

    def drain_left(j, carry):
        left_copy(j // chunks, lax.rem(j, chunks)).wait_send()
        return carry

    lax.fori_loop(0, n_right * chunks, drain_right, 0)
    lax.fori_loop(0, n_left * chunks, drain_left, 0)
    for k, (src, dst) in enumerate(((inp_ref, ginp_ref), (cot_ref, gcot_ref))):
        dp_copy(3 * k, src, dst, group, cross).wait_send()
        dp_copy(3 * k + 1, src, dst, group, sibling).wait_send()
        dp_copy(3 * k + 1, src, dst, sibling, sibling).wait_recv()
        dp_copy(3 * k + 2, dst.at[cross], dst, cross, sibling).wait_send()
        dp_copy(3 * k + 2, dst.at[cross], dst, far, sibling).wait_recv()
        pltpu.make_async_copy(src, dst.at[group], own_sem.at[k]).wait()
    for c in range(chunks):
        pltpu.make_async_copy(
            out_v.at[c], share_ref.at[:, pl.ds(c * width, width)], out_sem.at[c]
        ).wait()


def exchange(n, inputs, cotangent, weight):
    rows, feat = inputs.shape
    width = min(512, feat)
    chunks = feat // width
    slots = n - 1
    ring = pltpu.VMEM((slots, chunks, rows, width), jnp.bfloat16)
    sems = pltpu.SemaphoreType.DMA((slots, chunks))
    return pl.pallas_call(
        functools.partial(exchange_kernel, n, chunks),
        out_shape=(
            jax.ShapeDtypeStruct((rows, feat), jnp.float32),
            jax.ShapeDtypeStruct((4, rows, feat), jnp.bfloat16),
            jax.ShapeDtypeStruct((4, rows, feat), jnp.bfloat16),
        ),
        in_specs=[pl.BlockSpec(memory_space=pl.ANY)] * 3,
        out_specs=(pl.BlockSpec(memory_space=pl.ANY),) * 3,
        scratch_shapes=[
            pltpu.VMEM((rows, cotangent.shape[1]), jnp.bfloat16),
            pltpu.VMEM((2, width, weight.shape[1]), jnp.bfloat16),
            pltpu.VMEM((rows, width), jnp.float32),
            ring,
            ring,
            pltpu.VMEM((chunks, rows, width), jnp.float32),
            pltpu.SemaphoreType.DMA((2,)),
            pltpu.SemaphoreType.DMA,
            pltpu.SemaphoreType.DMA((chunks,)),
            pltpu.SemaphoreType.DMA((2,)),
            sems, sems, sems, sems,
            pltpu.SemaphoreType.DMA((6,)),
            pltpu.SemaphoreType.DMA((6,)),
        ],
        compiler_params=pltpu.CompilerParams(
            collective_id=0, has_side_effects=True, vmem_limit_bytes=40 * 1024 * 1024
        ),
        cost_estimate=pl.CostEstimate(
            flops=2 * rows * cotangent.shape[1] * weight.shape[0],
            bytes_accessed=400 * 1024 * 1024, transcendentals=0,
        ),
    )(cotangent, inputs, weight)


def fold_columns(values, match):
    width = values.shape[1]
    kept = jnp.where(match, values, 0.0)
    return sum(kept[:, i : i + LANES] for i in range(0, width, LANES))


def spread_columns(folded, match):
    repeats = match.shape[1] // LANES
    return jnp.where(match, jnp.concatenate([folded] * repeats, axis=1), jnp.zeros((), folded.dtype))


def local(inputs, cotangent, weight, down_weight_maps, up_weight_maps, counts, ranks, owners):
    slot_count, feature_local = inputs.shape
    group_count = counts.shape[0]
    width = down_weight_maps.shape[1]
    column = jnp.arange(width, dtype=jnp.int32)
    col_trial = column // LARGEST_RANK
    column_slot = column % LARGEST_RANK
    trial_ids = jnp.arange(TRIALS, dtype=jnp.int32)
    matches = col_trial[:, None] == trial_ids[None, :]
    rank_per_column = jnp.sum(jnp.where(matches, ranks[None, :], 0), axis=1)
    owner_col = jnp.sum(jnp.where(matches, owners[None, :], 0), axis=1)
    scale_per_column = jnp.where(
        column_slot < rank_per_column, adapter_alpha / rank_per_column.astype(jnp.float32), 0.0
    )
    trial_rows = jnp.sum(counts, axis=0)
    per_trial = 1.0 / jnp.maximum(trial_rows, 1).astype(jnp.float32)
    inverse_col = jnp.sum(jnp.where(matches, per_trial[None, :], 0.0), axis=1)
    cumulative = jnp.cumsum(counts, axis=1)
    group_ids = jnp.arange(group_count, dtype=jnp.int32)
    my_group = lax.axis_index("dp")
    positions = jnp.arange(slot_count, dtype=jnp.int32)
    trial_all = jnp.sum(
        (positions[None, :, None] >= cumulative[:, None, :]).astype(jnp.int32), axis=2
    )
    row_trial = jnp.sum(jnp.where((group_ids == my_group)[:, None], trial_all, 0), axis=0)
    is_live = row_trial < TRIALS
    match = row_trial[:, None] == col_trial[None, :]
    match_all = trial_all.reshape(-1)[:, None] == col_trial[None, :]
    coef = jnp.where(match, scale_per_column[None, :], 0.0)
    coef_folded = fold_columns(coef, match)

    down_part = jnp.dot(inputs, down_weight_maps, preferred_element_type=jnp.float32)
    back_part = lax.dot_general(
        cotangent, up_weight_maps, TRAILING, preferred_element_type=jnp.float32
    )
    folded = jnp.concatenate([fold_columns(down_part, match), fold_columns(back_part, match)], axis=1)
    folded = lax.psum(folded, "tensor")
    scaled_down_f = (coef_folded * folded[:, :LANES]).astype(jnp.bfloat16)
    scaled_back_f = (coef_folded * folded[:, LANES:]).astype(jnp.bfloat16)

    all_inputs = lax.all_gather(inputs, "tensor", axis=1, tiled=True)
    frozen_share, group_inputs, group_cotangent = exchange(
        lax.axis_size("tensor"), inputs, cotangent, weight
    )
    group_inputs = group_inputs.reshape(-1, feature_local)
    group_cotangent = group_cotangent.reshape(-1, cotangent.shape[1])
    both = lax.all_gather(
        jnp.concatenate([scaled_down_f, scaled_back_f], axis=1), "dp", axis=0, tiled=True
    )

    frozen_output = jnp.dot(all_inputs, weight, preferred_element_type=jnp.float32)
    scaled_down = spread_columns(scaled_down_f, match)
    scaled_back = spread_columns(scaled_back_f, match)
    merged = frozen_output + jnp.dot(scaled_down, up_weight_maps, preferred_element_type=jnp.float32)
    projected = jnp.where(is_live[:, None], merged, 0.0).astype(jnp.bfloat16)
    adapter_in = lax.dot_general(
        scaled_back, down_weight_maps, TRAILING, preferred_element_type=jnp.float32
    )
    input_grad = jnp.where(
        is_live[:, None], frozen_share + adapter_in, 0.0
    ).astype(jnp.bfloat16)

    owned = jnp.where(owner_col == my_group, inverse_col, 0.0)
    down_all = spread_columns(both[:, :LANES], match_all)
    back_all = spread_columns(both[:, LANES:], match_all)
    grad_a = lax.dot_general(group_inputs, back_all, FIRST, preferred_element_type=jnp.float32)
    grad_b = lax.dot_general(down_all, group_cotangent, FIRST, preferred_element_type=jnp.float32)
    grad_a = (grad_a * owned[None, :])[None]
    grad_b = (grad_b * owned[:, None])[None]
    return (projected, input_grad, grad_a, grad_b)


def solution(mesh):
    return jax.shard_map(
        local,
        mesh=mesh,
        in_specs=(
            P(("parts", "dp"), "tensor"),
            P(("parts", "dp"), "tensor"),
            P(None, "tensor"),
            P("tensor", "parts"),
            P("parts", "tensor"),
            P("parts", None),
            P("parts"),
            P("parts"),
        ),
        out_specs=(
            P(("parts", "dp"), "tensor"),
            P(("parts", "dp"), "tensor"),
            P(("parts", "dp"), "tensor", None),
            P(("parts", "dp"), None, "tensor"),
        ),
        check_vma=False,
    )
```

```python
import functools

import jax
import jax.numpy as jnp
from jax import lax
from jax.experimental import pallas as pl
from jax.experimental.pallas import tpu as pltpu
from jax.sharding import PartitionSpec as P

LARGEST_RANK = 64
TRIALS = 16
LANES = 128

adapter_alpha = 16.0

TRAILING = (((1,), (1,)), ((), ()))
FIRST = (((0,), (0,)), ((), ()))


MESH = pl.DeviceIdType.MESH


def exchange_kernel(
    n, chunks, cot_ref, inp_ref, w_ref, share_ref, front_ref, ginp_ref, gcot_ref,
    cot_v, wbuf, part, to_right, to_left, out_v, x_v, fbuf, acc,
    w_sem, cot_sem, out_sem, own_sem, rs_send, rs_recv, ls_send, ls_recv, dp_send, dp_recv,
    x_sem, f_sem, acc_sem, xr_send, xr_recv, xl_send, xl_recv,
):
    me = lax.axis_index("tensor")
    group = lax.axis_index("dp")
    sibling = group + 1 - 2 * lax.rem(group, 2)
    cross = lax.rem(group + 2, 4)
    far = lax.rem(sibling + 2, 4)
    right, left = jnp.minimum(me + 1, n - 1), jnp.maximum(me - 1, 0)
    n_right, n_left = n - 1 - me, me
    width = wbuf.shape[1]
    rows = cot_v.shape[0]
    feat = width * chunks

    def weight_copy(i):
        dest, _, c, _ = item(i)
        start = pl.multiple_of(dest * feat + c * width, width)
        return pltpu.make_async_copy(
            w_ref.at[pl.ds(start, width), :], wbuf.at[lax.rem(i, 2)], w_sem.at[lax.rem(i, 2)]
        )

    def item(i):
        both = jnp.minimum(n_right, n_left)
        paired = 2 * both * chunks
        in_pair = i < paired
        rest = jnp.maximum(i - paired, 0)
        p = jnp.where(in_pair, i // (2 * chunks), both + rest // chunks)
        c = jnp.where(in_pair, lax.rem(i, 2 * chunks) // 2, lax.rem(rest, chunks))
        is_right = jnp.where(in_pair, lax.rem(i, 2), jnp.where(n_right > n_left, 0, 1))
        own = i >= (n - 1) * chunks
        kind = jnp.where(own, 2, is_right)
        dest = jnp.where(own, me, jnp.where(is_right == 0, n - 1 - p, p))
        return dest, p, c, kind

    pltpu.make_async_copy(inp_ref, x_v.at[me], x_sem).start()
    pltpu.make_async_copy(cot_ref, cot_v, cot_sem).start()
    weight_copy(0).start()

    barrier = pltpu.get_barrier_semaphore()
    for peer in (sibling, cross):
        pl.semaphore_signal(barrier, inc=1, device_id={"dp": peer}, device_id_type=MESH)

    @pl.when(me > 0)
    def _():
        pl.semaphore_signal(barrier, inc=1, device_id={"tensor": left}, device_id_type=MESH)

    @pl.when(me < n - 1)
    def _():
        pl.semaphore_signal(barrier, inc=1, device_id={"tensor": right}, device_id_type=MESH)

    edges = jnp.where(me > 0, 1, 0) + jnp.where(me < n - 1, 1, 0)
    pl.semaphore_wait(barrier, 2 + edges)

    def dp_copy(k, src, dst, slot, peer):
        return pltpu.make_async_remote_copy(
            src_ref=src, dst_ref=dst.at[slot], send_sem=dp_send.at[k], recv_sem=dp_recv.at[k],
            device_id={"dp": peer}, device_id_type=MESH,
        )

    def right_copy(p, c):
        return pltpu.make_async_remote_copy(
            src_ref=to_right.at[p, c], dst_ref=to_right.at[p, c],
            send_sem=rs_send.at[p, c], recv_sem=rs_recv.at[p, c],
            device_id={"tensor": right}, device_id_type=MESH,
        )

    def left_copy(p, c):
        return pltpu.make_async_remote_copy(
            src_ref=to_left.at[p, c], dst_ref=to_left.at[p, c],
            send_sem=ls_send.at[p, c], recv_sem=ls_recv.at[p, c],
            device_id={"tensor": left}, device_id_type=MESH,
        )

    def pass_right(r):
        block = jnp.maximum(me - r, 0)
        return pltpu.make_async_remote_copy(
            src_ref=x_v.at[block], dst_ref=x_v.at[block],
            send_sem=xr_send.at[r], recv_sem=xr_recv.at[r],
            device_id={"tensor": right}, device_id_type=MESH,
        )

    def pass_left(r):
        block = jnp.minimum(me + r, n - 1)
        return pltpu.make_async_remote_copy(
            src_ref=x_v.at[block], dst_ref=x_v.at[block],
            send_sem=xl_send.at[r], recv_sem=xl_recv.at[r],
            device_id={"tensor": left}, device_id_type=MESH,
        )

    def front_copy(block, c):
        start = pl.multiple_of(block * feat + c * width, width)
        return pltpu.make_async_copy(
            w_ref.at[pl.ds(start, width), :], fbuf.at[lax.rem(c, 2)], f_sem.at[lax.rem(c, 2)]
        )

    def front(block):
        front_copy(block, 0).start()

        def chunk(c, carry):
            front_copy(block, c).wait()

            @pl.when(c + 1 < chunks)
            def _():
                front_copy(block, c + 1).start()

            columns = pl.ds(pl.multiple_of(c * width, width), width)

            def rows_of(h, inner):
                at = pl.ds(pl.multiple_of(h * tall, tall), tall)
                acc[at, :] += jnp.dot(
                    x_v[block, at, columns], fbuf[lax.rem(c, 2)],
                    preferred_element_type=jnp.float32,
                )
                return inner

            lax.fori_loop(0, rows // tall, rows_of, 0)
            return carry

        lax.fori_loop(0, chunks, chunk, 0)

    tall = rows // 2
    pltpu.make_async_copy(inp_ref, x_v.at[me], x_sem).wait()

    @pl.when(me < n - 1)
    def _():
        pass_right(0).start()

    @pl.when(me > 0)
    def _():
        pass_left(0).start()

    for k, (src, dst) in enumerate(((inp_ref, ginp_ref), (cot_ref, gcot_ref))):
        pltpu.make_async_copy(src, dst.at[group], own_sem.at[k]).start()
        dp_copy(3 * k, src, dst, group, cross).start()
        dp_copy(3 * k + 1, src, dst, group, sibling).start()

    pltpu.make_async_copy(cot_ref, cot_v, cot_sem).wait()

    def step(i, carry):
        dest, p, c, kind = item(i)
        weight_copy(i).wait()

        @pl.when(i + 1 < n * chunks)
        def _():
            weight_copy(i + 1).start()

        part[...] = lax.dot_general(
            cot_v[...], wbuf[lax.rem(i, 2)], TRAILING, preferred_element_type=jnp.float32
        )

        @pl.when(kind == 0)
        def _():
            @pl.when(me > 0)
            def _():
                right_copy(p, c).wait_recv()
                part[...] += to_right[p, c].astype(jnp.float32)

            to_right[p, c] = part[...].astype(jnp.bfloat16)
            right_copy(p, c).start()

        @pl.when(kind == 1)
        def _():
            @pl.when(me < n - 1)
            def _():
                left_copy(p, c).wait_recv()
                part[...] += to_left[p, c].astype(jnp.float32)

            to_left[p, c] = part[...].astype(jnp.bfloat16)
            left_copy(p, c).start()

        @pl.when(kind == 2)
        def _():
            @pl.when(me > 0)
            def _():
                right_copy(n_right, c).wait_recv()
                part[...] += to_right[n_right, c].astype(jnp.float32)

            @pl.when(me < n - 1)
            def _():
                left_copy(n_left, c).wait_recv()
                part[...] += to_left[n_left, c].astype(jnp.float32)

            out_v[c] = part[...]
            start = pl.multiple_of(c * width, width)
            pltpu.make_async_copy(
                out_v.at[c], share_ref.at[:, pl.ds(start, width)], out_sem.at[c]
            ).start()

        return carry

    acc[...] = jnp.zeros_like(acc)
    lax.fori_loop(0, chunks, step, 0)
    front(me)

    def turn(r, carry):
        from_left, from_right = r <= me, r <= n_right

        @pl.when(from_left)
        def _():
            pass_right(r - 1).wait_recv()

            @pl.when(me < n - 1)
            def _():
                pass_right(r).start()

        @pl.when(from_right)
        def _():
            pass_left(r - 1).wait_recv()

            @pl.when(me > 0)
            def _():
                pass_left(r).start()

        @pl.when(r < n - 1)
        def _():
            lax.fori_loop(r * chunks, (r + 1) * chunks, step, 0)

        @pl.when(from_left)
        def _():
            front(jnp.maximum(me - r, 0))

        @pl.when(from_right)
        def _():
            front(jnp.minimum(me + r, n - 1))

        return carry

    lax.fori_loop(1, n, turn, 0)
    pltpu.make_async_copy(acc, front_ref, acc_sem).start()

    for k, (src, dst) in enumerate(((inp_ref, ginp_ref), (cot_ref, gcot_ref))):
        dp_copy(3 * k, src, dst, cross, cross).wait_recv()
        dp_copy(3 * k + 2, dst.at[cross], dst, cross, sibling).start()

    lax.fori_loop((n - 1) * chunks, n * chunks, step, 0)

    def drain_right(j, carry):
        right_copy(j // chunks, lax.rem(j, chunks)).wait_send()
        return carry

    def drain_left(j, carry):
        left_copy(j // chunks, lax.rem(j, chunks)).wait_send()
        return carry

    def drain_pass_right(r, carry):
        pass_right(r).wait_send()
        return carry

    def drain_pass_left(r, carry):
        pass_left(r).wait_send()
        return carry

    @pl.when(me < n - 1)
    def _():
        lax.fori_loop(0, me + 1, drain_pass_right, 0)

    @pl.when(me > 0)
    def _():
        lax.fori_loop(0, n_right + 1, drain_pass_left, 0)

    pltpu.make_async_copy(acc, front_ref, acc_sem).wait()
    lax.fori_loop(0, n_right * chunks, drain_right, 0)
    lax.fori_loop(0, n_left * chunks, drain_left, 0)
    for k, (src, dst) in enumerate(((inp_ref, ginp_ref), (cot_ref, gcot_ref))):
        dp_copy(3 * k, src, dst, group, cross).wait_send()
        dp_copy(3 * k + 1, src, dst, group, sibling).wait_send()
        dp_copy(3 * k + 1, src, dst, sibling, sibling).wait_recv()
        dp_copy(3 * k + 2, dst.at[cross], dst, cross, sibling).wait_send()
        dp_copy(3 * k + 2, dst.at[cross], dst, far, sibling).wait_recv()
        pltpu.make_async_copy(src, dst.at[group], own_sem.at[k]).wait()
    for c in range(chunks):
        pltpu.make_async_copy(
            out_v.at[c], share_ref.at[:, pl.ds(c * width, width)], out_sem.at[c]
        ).wait()


def exchange(n, inputs, cotangent, weight):
    rows, feat = inputs.shape
    width = min(512, feat)
    chunks = feat // width
    slots = n - 1
    ring = pltpu.VMEM((slots, chunks, rows, width), jnp.bfloat16)
    sems = pltpu.SemaphoreType.DMA((slots, chunks))
    return pl.pallas_call(
        functools.partial(exchange_kernel, n, chunks),
        out_shape=(
            jax.ShapeDtypeStruct((rows, feat), jnp.float32),
            jax.ShapeDtypeStruct((rows, weight.shape[1]), jnp.float32),
            jax.ShapeDtypeStruct((4, rows, feat), jnp.bfloat16),
            jax.ShapeDtypeStruct((4, rows, feat), jnp.bfloat16),
        ),
        in_specs=[pl.BlockSpec(memory_space=pl.ANY)] * 3,
        out_specs=(pl.BlockSpec(memory_space=pl.ANY),) * 4,
        scratch_shapes=[
            pltpu.VMEM((rows, cotangent.shape[1]), jnp.bfloat16),
            pltpu.VMEM((2, width, weight.shape[1]), jnp.bfloat16),
            pltpu.VMEM((rows, width), jnp.float32),
            ring,
            ring,
            pltpu.VMEM((chunks, rows, width), jnp.float32),
            pltpu.VMEM((n, rows, feat), jnp.bfloat16),
            pltpu.VMEM((2, width, weight.shape[1]), jnp.bfloat16),
            pltpu.VMEM((rows, weight.shape[1]), jnp.float32),
            pltpu.SemaphoreType.DMA((2,)),
            pltpu.SemaphoreType.DMA,
            pltpu.SemaphoreType.DMA((chunks,)),
            pltpu.SemaphoreType.DMA((2,)),
            sems, sems, sems, sems,
            pltpu.SemaphoreType.DMA((6,)),
            pltpu.SemaphoreType.DMA((6,)),
            pltpu.SemaphoreType.DMA,
            pltpu.SemaphoreType.DMA((2,)),
            pltpu.SemaphoreType.DMA,
            pltpu.SemaphoreType.DMA((slots,)),
            pltpu.SemaphoreType.DMA((slots,)),
            pltpu.SemaphoreType.DMA((slots,)),
            pltpu.SemaphoreType.DMA((slots,)),
        ],
        compiler_params=pltpu.CompilerParams(
            collective_id=0, has_side_effects=True, vmem_limit_bytes=50 * 1024 * 1024
        ),
        cost_estimate=pl.CostEstimate(
            flops=4 * rows * cotangent.shape[1] * weight.shape[0],
            bytes_accessed=400 * 1024 * 1024, transcendentals=0,
        ),
    )(cotangent, inputs, weight)


def fold_columns(values, match):
    width = values.shape[1]
    kept = jnp.where(match, values, 0.0)
    return sum(kept[:, i : i + LANES] for i in range(0, width, LANES))


def spread_columns(folded, match):
    repeats = match.shape[1] // LANES
    return jnp.where(match, jnp.concatenate([folded] * repeats, axis=1), jnp.zeros((), folded.dtype))


def local(inputs, cotangent, weight, down_weight_maps, up_weight_maps, counts, ranks, owners):
    slot_count, feature_local = inputs.shape
    group_count = counts.shape[0]
    width = down_weight_maps.shape[1]
    column = jnp.arange(width, dtype=jnp.int32)
    col_trial = column // LARGEST_RANK
    column_slot = column % LARGEST_RANK
    trial_ids = jnp.arange(TRIALS, dtype=jnp.int32)
    matches = col_trial[:, None] == trial_ids[None, :]
    rank_per_column = jnp.sum(jnp.where(matches, ranks[None, :], 0), axis=1)
    owner_col = jnp.sum(jnp.where(matches, owners[None, :], 0), axis=1)
    scale_per_column = jnp.where(
        column_slot < rank_per_column, adapter_alpha / rank_per_column.astype(jnp.float32), 0.0
    )
    trial_rows = jnp.sum(counts, axis=0)
    per_trial = 1.0 / jnp.maximum(trial_rows, 1).astype(jnp.float32)
    inverse_col = jnp.sum(jnp.where(matches, per_trial[None, :], 0.0), axis=1)
    cumulative = jnp.cumsum(counts, axis=1)
    group_ids = jnp.arange(group_count, dtype=jnp.int32)
    my_group = lax.axis_index("dp")
    positions = jnp.arange(slot_count, dtype=jnp.int32)
    trial_all = jnp.sum(
        (positions[None, :, None] >= cumulative[:, None, :]).astype(jnp.int32), axis=2
    )
    row_trial = jnp.sum(jnp.where((group_ids == my_group)[:, None], trial_all, 0), axis=0)
    is_live = row_trial < TRIALS
    match = row_trial[:, None] == col_trial[None, :]
    match_all = trial_all.reshape(-1)[:, None] == col_trial[None, :]
    coef = jnp.where(match, scale_per_column[None, :], 0.0)
    coef_folded = fold_columns(coef, match)

    down_part = jnp.dot(inputs, down_weight_maps, preferred_element_type=jnp.float32)
    back_part = lax.dot_general(
        cotangent, up_weight_maps, TRAILING, preferred_element_type=jnp.float32
    )
    folded = jnp.concatenate([fold_columns(down_part, match), fold_columns(back_part, match)], axis=1)
    folded = lax.psum(folded, "tensor")
    scaled_down_f = (coef_folded * folded[:, :LANES]).astype(jnp.bfloat16)
    scaled_back_f = (coef_folded * folded[:, LANES:]).astype(jnp.bfloat16)

    frozen_share, frozen_output, group_inputs, group_cotangent = exchange(
        lax.axis_size("tensor"), inputs, cotangent, weight
    )
    group_inputs = group_inputs.reshape(-1, feature_local)
    group_cotangent = group_cotangent.reshape(-1, cotangent.shape[1])
    both = lax.all_gather(
        jnp.concatenate([scaled_down_f, scaled_back_f], axis=1), "dp", axis=0, tiled=True
    )

    scaled_down = spread_columns(scaled_down_f, match)
    scaled_back = spread_columns(scaled_back_f, match)
    merged = frozen_output + jnp.dot(scaled_down, up_weight_maps, preferred_element_type=jnp.float32)
    projected = jnp.where(is_live[:, None], merged, 0.0).astype(jnp.bfloat16)
    adapter_in = lax.dot_general(
        scaled_back, down_weight_maps, TRAILING, preferred_element_type=jnp.float32
    )
    input_grad = jnp.where(
        is_live[:, None], frozen_share + adapter_in, 0.0
    ).astype(jnp.bfloat16)

    owned = jnp.where(owner_col == my_group, inverse_col, 0.0)
    down_all = spread_columns(both[:, :LANES], match_all)
    back_all = spread_columns(both[:, LANES:], match_all)
    grad_a = lax.dot_general(group_inputs, back_all, FIRST, preferred_element_type=jnp.float32)
    grad_b = lax.dot_general(down_all, group_cotangent, FIRST, preferred_element_type=jnp.float32)
    grad_a = (grad_a * owned[None, :])[None]
    grad_b = (grad_b * owned[:, None])[None]
    return (projected, input_grad, grad_a, grad_b)


def solution(mesh):
    return jax.shard_map(
        local,
        mesh=mesh,
        in_specs=(
            P(("parts", "dp"), "tensor"),
            P(("parts", "dp"), "tensor"),
            P(None, "tensor"),
            P("tensor", "parts"),
            P("parts", "tensor"),
            P("parts", None),
            P("parts"),
            P("parts"),
        ),
        out_specs=(
            P(("parts", "dp"), "tensor"),
            P(("parts", "dp"), "tensor"),
            P(("parts", "dp"), "tensor", None),
            P(("parts", "dp"), None, "tensor"),
        ),
        check_vma=False,
    )
```
